32 devices in a mesh: row: 4 (over y, core), col: 8 (over z, x).
Axes of the slice: x: 2, y: 2, z: 4, core: 2. Of those that a mesh axis runs over, the one named last changes fastest.
Arguments:
- states_now: float32 [40, 4096], P(None, ('col', 'row')), may hold values from -60 to 60
- states_next: float32 [40, 4096], P(None, ('row', 'col')), may hold values from -60 to 60
- states_last: float32 [40, 4096], P(None, ('col', 'row')), may hold values from -60 to 60
- payoff_now: bfloat16 [64, 4096], P(None, ('col', 'row')), may hold values from 0 to 2
- payoff_next: bfloat16 [64, 4096], P(None, ('row', 'col')), may hold values from 0 to 2
- payoff_last: bfloat16 [64, 4096], P(None, ('col', 'row')), may hold values from 0 to 2
Outputs:
- value_next: float32 [64, 4096], P(None, ('row', 'col'))
- value_now: float32 [64, 4096], P(None, ('col', 'row'))
The draws below stay inside these ranges and needn't reach their ends.
All inputs are finite; a program needn't handle non-finite values.
Results may differ from the reference program's by a relative error of at most 0.0003.
Values sent between devices are 32-bit elements; how exact they have to be, the bound alone decides.
No kernel may reach another device: no remote copies, remote signals or barrier semaphores. Data moves between devices by JAX's collectives and lax.ppermute only.
A program may use at most 128 MiB of HBM per device.

```python
import math
import jax
import jax.numpy as jnp
from jax import lax

F = 40
SWAPS = 64
MESH_PTS = 4096


def draw_mesh(key):
    grid_shape = (3, F, MESH_PTS)
    points = 0.55 * jax.random.truncated_normal(jax.random.fold_in(key, 7), -6.0, 6.0, grid_shape, jnp.float32)
    return points


def draw_states_now(key, part):
    return draw_mesh(key)[0]


def draw_states_next(key, part):
    return draw_mesh(key)[1]


def draw_states_last(key, part):
    return draw_mesh(key)[2]


def levels(rng, dims, cuts, smallest, largest):
    factor_of, own = 1.0, jax.random.fold_in(rng, 6)
    for axis_at, shards_of in cuts:
        draws = jnp.exp(jax.random.uniform(jax.random.fold_in(own, axis_at), (shards_of,), jnp.float32, smallest / len(cuts), largest / len(cuts)))
        factor_of = factor_of * jnp.repeat(draws, dims[axis_at] // shards_of).reshape([-1 if axis == axis_at else 1 for axis in range(len(dims))])
    return factor_of


def setup_inputs(seed: int = 0) -> dict:
    seeds = jax.random.split(jax.random.key(seed), 7)
    return {
        "states_now": draw_states_now(jax.random.fold_in(seeds[6], 71), 0),
        "states_next": draw_states_next(jax.random.fold_in(seeds[6], 71), 0),
        "states_last": draw_states_last(jax.random.fold_in(seeds[6], 71), 0),
        "payoff_now": jnp.clip(2.0 * jax.random.uniform(seeds[3], (SWAPS, MESH_PTS), jnp.float32) ** levels(seeds[3], (SWAPS, MESH_PTS), ((1, 32),), -0.2, 0.2), 0.0, 2.0).astype(jnp.bfloat16),
        "payoff_next": jnp.clip(2.0 * jax.random.uniform(seeds[4], (SWAPS, MESH_PTS), jnp.float32) ** levels(seeds[4], (SWAPS, MESH_PTS), ((1, 32),), -0.2, 0.2), 0.0, 2.0).astype(jnp.bfloat16),
        "payoff_last": jnp.clip(2.0 * jax.random.uniform(seeds[5], (SWAPS, MESH_PTS), jnp.float32) ** levels(seeds[5], (SWAPS, MESH_PTS), ((1, 32),), -0.2, 0.2), 0.0, 2.0).astype(jnp.bfloat16),
    }


def backward(earlier, later, later_value, payoff):
    factors, points = earlier.shape
    swaps = later_value.shape[0]
    block_cols = math.gcd(points, 1024)
    block_count = points // block_cols
    row_norms = jnp.sum(earlier * earlier, axis=0)
    col_blocks = later.reshape(factors, block_count, block_cols).transpose(1, 0, 2)
    value_blocks = later_value.reshape(swaps, block_count, block_cols).transpose(1, 0, 2)

    def update(running, block_item):
        col_states, col_values = block_item
        col_norms = jnp.sum(col_states * col_states, axis=0)
        cross_term = jnp.dot(earlier.T, col_states, precision=lax.Precision.HIGHEST, preferred_element_type=jnp.float32)
        log_weight = cross_term - 0.5 * row_norms[:, None] - 0.5 * col_norms[None, :]
        col_peak = jnp.max(log_weight, axis=0)
        shifted = jnp.exp(log_weight - col_peak[None, :])
        density = jnp.sum(shifted, axis=0)
        kernel = shifted.astype(jnp.bfloat16)
        scaled = (col_values / density[None, :]).astype(jnp.bfloat16)
        return running + jnp.dot(scaled, kernel.T, preferred_element_type=jnp.float32), None

    initial = jnp.zeros((swaps, points), jnp.float32)
    continuation, ignored = lax.scan(update, initial, (col_blocks, value_blocks))
    return jnp.maximum(payoff.astype(jnp.float32), continuation)


def reference(states_now, states_next, states_last, payoff_now, payoff_next, payoff_last):
    value_next = backward(states_next, states_last, payoff_last.astype(jnp.float32), payoff_next)
    value_now = backward(states_now, states_next, value_next, payoff_now)
    return value_next, value_now
```

```python
import functools

import jax
import jax.numpy as jnp
from jax import lax
from jax.experimental import pallas as pl
from jax.experimental.pallas import tpu as pltpu
from jax.sharding import PartitionSpec as P

LANES = 128
SPLIT_ROWS = 8


def swapped(array, link):
    axis, bit = link
    pairs = [(i, i ^ bit) for i in range(lax.axis_size(axis))]
    return lax.ppermute(array, axis, pairs)


def bits(axis, lowest, end):
    size = lax.axis_size(axis)
    return [(axis, 1 << k) for k in range(lowest, size.bit_length() - 1) if (1 << k) < end]


def gathered(block, links):
    for link in links:
        block = jnp.concatenate([block, swapped(block, link)], axis=0)
    return block


def flipped(array, level):
    count = array.shape[0]
    step = 1 << level
    shape = (count // (2 * step), 2, step) + array.shape[1:]
    return jnp.flip(array.reshape(shape), axis=1).reshape(array.shape)


def summed(array, links):
    for level, link in enumerate(links):
        array = array + flipped(swapped(array, link), level)
    return array


def scattered(array, links):
    for link in reversed(links):
        half = array.shape[0] // 2
        array = array[:half] + swapped(array[half:], link)
    return array


def joined_stats(stats, links):
    for level, link in reversed(list(enumerate(links))):
        other = flipped(swapped(stats, link), level)
        peak = jnp.maximum(stats[:, :1], other[:, :1])
        total = stats[:, 1:] * jnp.exp(stats[:, :1] - peak) + other[:, 1:] * jnp.exp(other[:, :1] - peak)
        stats = jnp.concatenate([peak, total], axis=1)
    return stats


def thirds(x):
    high = x.astype(jnp.bfloat16).astype(jnp.float32)
    rest = x - high
    middle = rest.astype(jnp.bfloat16).astype(jnp.float32)
    return high, middle, rest - middle


def operand(states, earlier):
    high, middle, low = thirds(states)
    norm = thirds(-0.5 * jnp.sum(states * states, axis=0, keepdims=True))
    lanes = states.shape[1]
    row = lax.broadcasted_iota(jnp.int32, (SPLIT_ROWS, lanes), 0)
    first = 0 if earlier else 3
    tail = jnp.where(row < 6, 1.0, 0.0)
    for k in range(3):
        tail = jnp.where(row == first + k, norm[k], tail)
    if earlier:
        parts = [high, high, middle, middle, high, low, tail]
    else:
        parts = [high, middle, high, middle, low, high, tail]
    return jnp.concatenate(parts, axis=0).astype(jnp.bfloat16)


def weights_kernel(earlier_ref, later_ref, weight_ref, stats_ref):
    rows = jnp.concatenate([operand(earlier_ref[b], True) for b in range(earlier_ref.shape[0])], axis=1)
    width = weight_ref.shape[2]
    per = width // LANES
    for c in range(weight_ref.shape[0]):
        cols = jnp.concatenate([operand(later_ref[c * per + b], False) for b in range(per)], axis=1)
        log_weight = lax.dot_general(rows, cols, (((0,), (0,)), ((), ())), preferred_element_type=jnp.float32)
        peak = jnp.max(log_weight, axis=0, keepdims=True)
        weight = jnp.exp(log_weight - peak)
        total = jnp.sum(weight, axis=0, keepdims=True)
        weight_ref[c] = weight
        for b in range(per):
            stats_ref[c * per + b, 0:1] = peak[:, b * LANES : (b + 1) * LANES]
            stats_ref[c * per + b, 1:2] = total[:, b * LANES : (b + 1) * LANES]


def weights(earlier, later):
    count, points = later.shape[0], earlier.shape[0] * LANES
    per = 2 if count % 2 == 0 else 1
    return pl.pallas_call(
        weights_kernel,
        out_shape=(
            jax.ShapeDtypeStruct((count // per, points, per * LANES), jnp.float32),
            jax.ShapeDtypeStruct((count, 2, LANES), jnp.float32),
        ),
        in_specs=[pl.BlockSpec(memory_space=pltpu.VMEM)] * 2,
        out_specs=(pl.BlockSpec(memory_space=pltpu.VMEM),) * 2,
        cost_estimate=pl.CostEstimate(
            flops=2 * 256 * points * count * LANES,
            bytes_accessed=4 * points * count * LANES,
            transcendentals=points * count * LANES,
        ),
        name="weights",
    )(earlier, later)


def project(weight_ref, local_ref, joined_ref, values, out_ref):
    total = None
    per = weight_ref.shape[2] // LANES
    for c in range(weight_ref.shape[0]):
        blocks = range(c * per, (c + 1) * per)
        scale = jnp.concatenate([jnp.exp(local_ref[b, 0:1] - joined_ref[b, 0:1]) for b in blocks], axis=1)
        scaled = jnp.concatenate([values(b) / joined_ref[b, 1:2] for b in blocks], axis=1).astype(jnp.bfloat16)
        kernel = (weight_ref[c] * scale).astype(jnp.bfloat16)
        term = lax.dot_general(scaled, kernel, (((1,), (1,)), ((), ())), preferred_element_type=jnp.float32)
        total = term if total is None else total + term
    for b in range(out_ref.shape[0]):
        out_ref[b] = total[:, b * LANES : (b + 1) * LANES]


def first_kernel(weight_ref, local_ref, joined_ref, value_ref, out_ref):
    project(weight_ref, local_ref, joined_ref, lambda b: value_ref[b], out_ref)


def second_kernel(weight_ref, local_ref, joined_ref, sum_ref, payoff_ref, out_ref, value_ref):
    value_ref[...] = jnp.maximum(payoff_ref[0], sum_ref[0])
    project(weight_ref, local_ref, joined_ref, lambda b: jnp.maximum(payoff_ref[b], sum_ref[b]), out_ref)


def continuation(weight, local, joined, *values):
    points = weight.shape[1]
    swaps = values[0].shape[1]
    out = jax.ShapeDtypeStruct((points // LANES, swaps, LANES), jnp.float32)
    second = len(values) == 2
    outs = (out, jax.ShapeDtypeStruct((swaps, LANES), jnp.float32)) if second else out
    vmem = pl.BlockSpec(memory_space=pltpu.VMEM)
    return pl.pallas_call(
        second_kernel if second else first_kernel,
        out_shape=outs,
        in_specs=[vmem] * (3 + len(values)),
        out_specs=(vmem, vmem) if second else vmem,
        cost_estimate=pl.CostEstimate(
            flops=2 * swaps * weight.size, bytes_accessed=4 * weight.size, transcendentals=weight.size // points
        ),
        name="project",
    )(weight, local, joined, *values)


def per_device(states_now, states_next, states_last, payoff_now, payoff_next, payoff_last):
    row_size, col_size = lax.axis_size("row"), lax.axis_size("col")
    far = list(reversed([("row", 1)] + bits("col", 1, col_size)))
    near = bits("row", 1, row_size) + bits("col", 0, 2)
    wide = jnp.float32
    last = gathered(states_last[None], far)
    following = gathered(states_next[None], near)
    weight1, local1 = weights(following, last)
    joined1 = joined_stats(local1, far)
    last_value = gathered(payoff_last.astype(wide)[None], far)
    sum1 = summed(continuation(weight1, local1, joined1, last_value), near)

    now = gathered(states_now[None], far)
    weight2, local2 = weights(now, following)
    joined2 = joined_stats(local2, near)
    next_payoff = gathered(payoff_next.astype(wide)[None], near)
    sum2, value_next = continuation(weight2, local2, joined2, sum1, next_payoff)
    value_now = jnp.maximum(payoff_now.astype(wide), scattered(sum2, far)[0])
    return (value_next, value_now)


def solution(mesh):
    in_specs = (
        P(None, ("col", "row")),
        P(None, ("row", "col")),
        P(None, ("col", "row")),
        P(None, ("col", "row")),
        P(None, ("row", "col")),
        P(None, ("col", "row")),
    )
    out_specs = (P(None, ("row", "col")), P(None, ("col", "row")))
    return jax.shard_map(per_device, mesh=mesh, in_specs=in_specs, out_specs=out_specs, check_vma=False)
```
